512 devices in a mesh: row: 16 (over y, x_hi), col: 16 (over z, core), rep: 2 (over x_lo).
Axes of the slice: x: 4 (x_hi: 2, x_lo: 2; x = x_hi * 2 + x_lo), y: 8, z: 8, core: 2. Of those that a mesh axis runs over, the one named last changes fastest.
Arguments:
- amplitudes: bfloat16 [64, 64, 6, 5184], P('row', 'col', 'rep'), may hold values from -6 to 6
- integrals: bfloat16 [5184, 6, 5184], P('col', 'rep', 'row'), may hold values from -0.03125 to 0.03125
- occ_offsets: int32 [9], replicated, may hold values from 0 to 64, as said below
- slab: int32 [2], replicated, may hold values from 0 to 7
Outputs:
- residual: bfloat16 [64, 64, 5184], P('row', 'col')
The draws below stay inside these ranges and needn't reach their ends.
Inputs may be any that keep to these rules, and one draw needn't show every extreme that they name: `occ_offsets`: never falling; entry 0 is 0 and entry 8 is 64; entries k and k+1 bound the occupied orbitals of irrep k.
All inputs are finite; a program needn't handle non-finite values.
Results may differ from the reference program's by a relative error of at most 0.02.
Values may be sent and summed in bfloat16 or wider, within the bound.
No kernel may reach another device: no remote copies, remote signals or barrier semaphores. Data moves between devices by JAX's collectives and lax.ppermute only.
A program may use at most 128 MiB of HBM per device.

```python
import jax
import jax.numpy as jnp
from jax import lax

KB = 6
O = 64
CDB = 5184
AB = 5184
N_ROW = 16
N_REP = 2


def draw_occ_offsets(key, part):
    inner = jnp.sort(jax.random.randint(key, (7,), 0, O + 1)).astype(jnp.int32)
    first = jnp.zeros((1,), jnp.int32)
    last = jnp.full((1,), O, jnp.int32)
    return jnp.concatenate([first, inner, last])


def steps_of(stream_key, shape, pieces, smallest, high):
    gain, own = 1.0, jax.random.fold_in(stream_key, 6)
    for dim, parts in pieces:
        steps = jnp.exp(jax.random.uniform(jax.random.fold_in(own, dim), (parts,), jnp.float32, smallest / len(pieces), high / len(pieces)))
        gain = gain * jnp.repeat(steps, shape[dim] // parts).reshape([-1 if axis == dim else 1 for axis in range(len(shape))])
    return gain


def normal_values(rng, shape, spread, reach, shards=(), kind=jnp.bfloat16):
    drawn = spread * jax.random.normal(rng, shape, jnp.float32)
    if shards:
        drawn = drawn * steps_of(rng, shape, shards, -0.22, 0.18)
    return jnp.clip(drawn, -reach, reach).astype(kind)


def setup_inputs(seed: int = 0) -> dict:
    arg_keys = jax.random.split(jax.random.key(seed), 5)
    amplitudes = normal_values(arg_keys[0], (O, O, KB, CDB), 1.0, 6.0, ((0, 16), (1, 16), (2, 2)))
    integrals = normal_values(arg_keys[1], (AB, KB, CDB), (KB * CDB) ** -0.5, 0.03125, ((0, 16), (1, 2), (2, 16)))
    occ_offsets = draw_occ_offsets(jax.random.fold_in(arg_keys[4], 71), 0)
    slab = jax.random.randint(arg_keys[3], (2,), 0, 8).astype(jnp.int32)
    return dict(amplitudes=amplitudes, integrals=integrals, occ_offsets=occ_offsets, slab=slab)


def irrep_labels(orbitals, occ_offsets):
    return jnp.sum((orbitals[:, None] >= occ_offsets[None, 1:8]).astype(jnp.int32), axis=1).astype(jnp.int32)


def reference(amplitudes, integrals, occ_offsets, slab):
    half_blocks = KB // N_REP
    sub_width = CDB // N_ROW
    blocked_amps = amplitudes.reshape(O, O, N_REP, half_blocks, N_ROW, sub_width)
    blocked_ints = integrals.reshape(AB, N_REP, half_blocks, N_ROW, sub_width)

    def accumulate(total, number):
        rep_part = number // N_ROW
        row_part = number % N_ROW
        amps = lax.dynamic_index_in_dim(blocked_amps, rep_part, 2, keepdims=False)
        amps = lax.dynamic_index_in_dim(amps, row_part, 3, keepdims=False)
        ints = lax.dynamic_index_in_dim(blocked_ints, rep_part, 1, keepdims=False)
        ints = lax.dynamic_index_in_dim(ints, row_part, 2, keepdims=False)
        partial_value = jnp.einsum('ijkc,akc->ija', amps.astype(jnp.float32), ints.astype(jnp.float32))
        rounded = lax.optimization_barrier(partial_value.astype(jnp.bfloat16))
        return total + rounded.astype(jnp.float32), None

    numbers = jnp.arange(N_REP * N_ROW, dtype=jnp.int32)
    total = lax.scan(accumulate, jnp.zeros((O, O, AB), jnp.float32), numbers)[0]
    ladder = lax.optimization_barrier(total.astype(jnp.bfloat16))
    orbitals = jnp.arange(O, dtype=jnp.int32)
    labels = irrep_labels(orbitals, occ_offsets)
    target = jnp.bitwise_xor(slab[0], slab[1])
    allowed = jnp.bitwise_xor(labels[:, None], labels[None, :]) == target
    wide = ladder.astype(jnp.float32)
    mixed = wide - jnp.swapaxes(wide, 0, 1)
    return jnp.where(allowed[:, :, None], mixed, jnp.float32(0.0)).astype(jnp.bfloat16)
```

```python
import functools

import jax
import jax.numpy as jnp
import numpy as np
from jax import lax
from jax.experimental import pallas as pl
from jax.experimental.pallas import tpu as pltpu
from jax.sharding import Mesh, PartitionSpec as P

BF = jnp.bfloat16
F32 = jnp.float32
AXES = ("y", "xh", "z", "core", "xl")
PLANE = ("y", "xh", "xl")
ROW = ("y", "xh")
VM = pl.BlockSpec(memory_space=pltpu.VMEM)
SM = pl.BlockSpec(memory_space=pltpu.SMEM)


def cost(flops, nbytes):
    return pl.CostEstimate(flops=flops, bytes_accessed=nbytes, transcendentals=0)


def pack_a_kernel(rows, sub, a_ref, o_ref):
    ni, nk, nj, _ = a_ref.shape
    for r in range(rows):
        for i in range(ni):
            piece = jnp.concatenate([a_ref[i, k, :, r * sub : (r + 1) * sub] for k in range(nk)], axis=1)
            for p in range(o_ref.shape[1]):
                o_ref[r, p, i * nj : (i + 1) * nj, :] = piece


def pack_b_kernel(half, p_ref, b_ref, keep_ref, send_ref):
    nk = b_ref.shape[0]
    full = jnp.concatenate([b_ref[k] for k in range(nk)], axis=1)
    low = full[:half]
    high = full[half:]
    first = p_ref[0] == 0

    @pl.when(first)
    def _():
        keep_ref[...] = low
        send_ref[...] = high

    @pl.when(jnp.logical_not(first))
    def _():
        keep_ref[...] = high
        send_ref[...] = low


def contract_kernel(blocks, core_ref, *refs):
    own0, own1, oth0, oth1 = refs[:4]
    subs = refs[4 : 4 + 2 * blocks]
    o_ref = refs[-1]
    core = core_ref[0]
    dims = (((1,), (1,)), ((), ()))
    rt, mi, kc = own0.shape
    for slot, (k0, k1) in ((core, (own0, own1)), (1 - core, (oth0, oth1))):
        lhs0 = k0[...].reshape(rt * mi, kc)
        lhs1 = k1[...].reshape(rt * mi, kc)
        parts = []
        for b in range(blocks):
            acc = lax.dot_general(lhs0, subs[2 * b][...], dims, preferred_element_type=F32)
            acc += lax.dot_general(lhs1, subs[2 * b + 1][...], dims, preferred_element_type=F32)
            parts.append(acc)
        full = parts[0] if blocks == 1 else jnp.concatenate(parts, axis=1)
        o_ref[:, pl.ds(slot, 1), :, :] = full.astype(BF).reshape(rt, 1, mi, full.shape[1])


def contract(core, amps, subs):
    blocks = len(subs) // 2
    rt, mi, kc = amps[0].shape
    half = subs[0].shape[0]
    width = blocks * half
    return pl.pallas_call(
        functools.partial(contract_kernel, blocks),
        in_specs=[SM] + [VM] * (4 + 2 * blocks),
        out_specs=VM,
        out_shape=jax.ShapeDtypeStruct((rt, 2, mi, width), BF),
        cost_estimate=cost(2 * 2 * rt * mi * 2 * kc * width, 2 * (4 * rt * mi * kc + width * 2 * kc + 2 * rt * mi * width)),
    )(core, *amps, *subs)


def total_of(x_ref, slot):
    acc = x_ref[0, slot].astype(F32)
    for s in range(1, x_ref.shape[0]):
        acc += x_ref[s, slot].astype(F32)
    return acc


def gather_sum_kernel(layout, half, idx_ref, *refs):
    chunks, outs = refs[: len(layout)], refs[len(layout) :]
    z, first = idx_ref[0], idx_ref[1]
    for s, o_ref in enumerate(outs):
        slot = first if s == 0 else 1 - first
        for x_ref, offs in zip(chunks, layout):
            total = total_of(x_ref, slot).astype(BF)
            for b, off in enumerate(offs):
                at = lax.rem(z + off + 8, 8)
                o_ref[pl.ds(at, 1)] = total[:, b * half : (b + 1) * half][None]


def antisym_kernel(idx_ref, occ_ref, slab_ref, s0_ref, s1_ref, m0_ref, m1_ref, o_ref):
    row, z, first = idx_ref[0], idx_ref[1], idx_ref[2]
    target = slab_ref[0] ^ slab_ref[1]
    n = s0_ref.shape[1]
    side = 4
    r = lax.broadcasted_iota(jnp.int32, (n, 1), 0)
    ri = lax.broadcasted_iota(jnp.int32, (n, n), 0)
    ci = lax.broadcasted_iota(jnp.int32, (n, n), 1)
    swap = jnp.where((ri // side == ci % side) & (ri % side == ci // side), 1.0, 0.0).astype(BF)
    for s, (s_ref, m_ref) in enumerate(((s0_ref, m0_ref), (s1_ref, m1_ref))):
        piece = first if s == 0 else 1 - first
        i_orb = row * side + r // side
        j_orb = (2 * z + piece) * side + r % side
        i_lab = jnp.zeros((n, 1), jnp.int32)
        j_lab = jnp.zeros((n, 1), jnp.int32)
        for k in range(1, 8):
            i_lab += (i_orb >= occ_ref[k]).astype(jnp.int32)
            j_lab += (j_orb >= occ_ref[k]).astype(jnp.int32)
        allowed = (i_lab ^ j_lab) == target
        for b in range(s_ref.shape[0]):
            flipped = jnp.dot(swap, m_ref[b], preferred_element_type=F32)
            mixed = s_ref[b].astype(F32) - flipped
            mixed = jnp.where(allowed, mixed, 0.0).astype(BF)
            o_ref[pl.ds(piece, 1), pl.ds(b, 1)] = mixed[None, None]


def assemble_kernel(half, idx_ref, x_ref, o_ref):
    nz = x_ref.shape[1]
    for i in range(o_ref.shape[0]):
        rows = slice(i * o_ref.shape[1], (i + 1) * o_ref.shape[1])
        parts = []
        for z in range(nz):
            for core in range(2):
                for xl in range(2):
                    parts.append(x_ref[core * 2 + xl, z, rows, :])
        o_ref[i] = jnp.concatenate(parts, axis=1)


def kernel_call(body, outs, in_specs, args, nbytes):
    many = isinstance(outs, (list, tuple))
    return pl.pallas_call(
        body,
        in_specs=in_specs,
        out_specs=[VM] * len(outs) if many else VM,
        out_shape=outs,
        cost_estimate=cost(nbytes, nbytes),
    )(*args)


def shards(amplitudes, integrals, occ_offsets, slab):
    ni, nj, nk, nc = amplitudes.shape
    na, _, sub = integrals.shape
    rows = nc // sub
    half = na // 2
    kc = nk * sub
    y, xh, z = lax.axis_index("y"), lax.axis_index("xh"), lax.axis_index("z")
    core, xl = lax.axis_index("core"), lax.axis_index("xl")
    core1 = core.astype(jnp.int32).reshape(1)

    keep, send = kernel_call(
        functools.partial(pack_b_kernel, half),
        [jax.ShapeDtypeStruct((half, kc), BF)] * 2,
        [SM, VM],
        (xl.astype(jnp.int32).reshape(1), jnp.transpose(integrals, (1, 0, 2))),
        4 * na * kc,
    )
    packed = kernel_call(
        functools.partial(pack_a_kernel, rows, sub),
        jax.ShapeDtypeStruct((rows, 2, ni * nj, kc), BF),
        [VM],
        (jnp.transpose(amplitudes, (0, 2, 1, 3)),),
        6 * ni * nj * nk * nc,
    )

    def shift(x, axis, by):
        n = lax.axis_size(axis)
        return lax.ppermute(x, axis, [(d, (d + by) % n) for d in range(n)])

    recv = shift(send, "xl", 1)
    up = {0: (keep, recv)}
    down = {0: (keep, recv)}
    for t in range(1, 4):
        up[t] = tuple(shift(v, "z", 1) for v in up[t - 1])
        down[t] = tuple(shift(v, "z", -1) for v in down[t - 1])
    far = (shift(up[3][0], "z", 1), shift(down[3][1], "z", -1))

    swapped = lax.all_to_all(
        packed.reshape(rows * 2, ni * nj, kc), PLANE, split_axis=0, concat_axis=0, tiled=True
    ).reshape(rows, 2, ni * nj, kc)
    other_core = shift(swapped, "core", 1)

    def by_k(v):
        pair = lax.dynamic_slice_in_dim(v, xl, 1, 1), lax.dynamic_slice_in_dim(v, 1 - xl, 1, 1)
        return [q.reshape(rows, ni * nj, kc) for q in pair]

    amps = by_k(swapped) + by_k(other_core)

    def reduce(part):
        return lax.all_to_all(part, ROW, split_axis=0, concat_axis=0, tiled=True)

    plan = (
        ((0, -1, 1, -2, 2), (up[0], up[1], down[1], up[2], down[2])),
        ((-3, 3, 4), (up[3], down[3], far)),
    )
    pieces = [reduce(contract(core1, amps, [q for pair in subs for q in pair])) for _, subs in plan]
    layout = [offs for offs, _ in plan]

    nz = lax.axis_size("z")
    n = ni * nj
    piece = jax.ShapeDtypeStruct((nz, n, half), BF)
    first = xh.astype(jnp.int32)
    s0, s1 = kernel_call(
        functools.partial(gather_sum_kernel, layout, half),
        [piece, piece],
        [SM] + [VM] * len(pieces),
        (jnp.stack([z.astype(jnp.int32), first]), *pieces),
        2 * 2 * rows * n * nz * half,
    )

    shape = tuple(lax.axis_size(a) for a in AXES)

    def mirror(x, s):
        pairs = []
        for at in np.ndindex(*shape):
            to = (at[2], at[1] ^ s, at[0], at[3], at[4])
            pairs.append((int(np.ravel_multi_index(at, shape)), int(np.ravel_multi_index(to, shape))))
        return lax.ppermute(x, AXES, pairs)

    m0, m1 = mirror(s0, 0), mirror(s1, 1)
    row = (y * 2 + xh).astype(jnp.int32)
    mixed = kernel_call(
        antisym_kernel,
        jax.ShapeDtypeStruct((2, nz, n, half), BF),
        [SM, SM, SM, VM, VM, VM, VM],
        (jnp.stack([row, z.astype(jnp.int32), first]), occ_offsets, slab, s0, s1, m0, m1),
        2 * 6 * nz * n * half,
    )
    both = jnp.broadcast_to(mixed[:, None], (2, 2, nz, n, half)).reshape(4, nz, n, half)
    final = lax.all_to_all(both, ("core", "xl"), split_axis=0, concat_axis=0, tiled=True)
    return kernel_call(
        functools.partial(assemble_kernel, half),
        jax.ShapeDtypeStruct((ni, nj, nz * 4 * half), BF),
        [SM, VM],
        (core1, final),
        2 * 8 * nz * n * half,
    )


def solution(mesh):
    fine = Mesh(mesh.devices.reshape(8, 2, 8, 2, 2), AXES)
    row, col = ("y", "xh"), ("z", "core")
    placed = (P(row, col, "xl", None), P(col, "xl", row), P(), P())
    return jax.shard_map(
        shards, mesh=fine, in_specs=placed, out_specs=P(row, col, None), check_vma=False
    )
```

```python
import functools

import jax
import jax.numpy as jnp
import numpy as np
from jax import lax
from jax.experimental import pallas as pl
from jax.experimental.pallas import tpu as pltpu
from jax.sharding import Mesh, PartitionSpec as P

BF = jnp.bfloat16
F32 = jnp.float32
AXES = ("y", "xh", "z", "core", "xl")
PLANE = ("y", "xh", "xl")
ROW = ("y", "xh")
TARGET = ("y", "xh", "core")
VM = pl.BlockSpec(memory_space=pltpu.VMEM)
SM = pl.BlockSpec(memory_space=pltpu.SMEM)


def cost(flops, nbytes):
    return pl.CostEstimate(flops=flops, bytes_accessed=nbytes, transcendentals=0)


def pack_a_kernel(rows, sub, a_ref, o_ref):
    ni, nk, nj, _ = a_ref.shape
    for r in range(rows):
        for i in range(ni):
            piece = jnp.concatenate([a_ref[i, k, :, r * sub : (r + 1) * sub] for k in range(nk)], axis=1)
            for p in range(o_ref.shape[1]):
                o_ref[r, p, i * nj : (i + 1) * nj, :] = piece


def pack_b_kernel(p_ref, b_ref, keep_ref, send_ref):
    full = jnp.concatenate([b_ref[k] for k in range(b_ref.shape[0])], axis=1)
    half = full.shape[0] // 2
    pad = jnp.zeros((keep_ref.shape[0] - half, full.shape[1]), full.dtype)
    low = jnp.concatenate([full[:half], pad], axis=0)
    high = jnp.concatenate([full[half:], pad], axis=0)
    first = p_ref[0] == 0

    @pl.when(first)
    def _():
        keep_ref[...] = low
        send_ref[...] = high

    @pl.when(jnp.logical_not(first))
    def _():
        keep_ref[...] = high
        send_ref[...] = low


def join_kernel(x_ref, y_ref, o_ref):
    o_ref[0] = x_ref[...]
    o_ref[1] = y_ref[...]


def contract_kernel(half, form, pos_ref, own_ref, oth_ref, *refs):
    o_ref = refs[-1]
    halves, at = [], 0
    for count in form:
        if count == 1:
            halves.append((refs[at][0], refs[at][1]))
        else:
            halves.append((refs[at][...], refs[at + 1][...]))
        at += count
    core, p = pos_ref[0], pos_ref[1]
    dims = (((1,), (1,)), ((), ()))
    rt, _, mi, kc = own_ref.shape
    for slot, ref in ((core, own_ref), (1 - core, oth_ref)):
        lhs = [ref[:, pl.ds(h, 1)].reshape(rt * mi, kc) for h in (p, 1 - p)]
        parts = []
        for rhs in halves:
            acc = lax.dot_general(lhs[0], rhs[0], dims, preferred_element_type=F32)
            acc += lax.dot_general(lhs[1], rhs[1], dims, preferred_element_type=F32)
            parts.append(acc[:, :half])
        full = parts[0] if len(parts) == 1 else jnp.concatenate(parts, axis=1)
        o_ref[:, pl.ds(slot, 1), :, :] = full.astype(BF).reshape(rt, 1, mi, full.shape[1])


def take_half_kernel(x_ref, o_ref):
    o_ref[...] = x_ref[0]


def take_half(x, p):
    _, half, kc = x.shape
    return pl.pallas_call(
        take_half_kernel,
        grid=(1,),
        in_specs=[pl.BlockSpec((1, half, kc), lambda s: (p, 0, 0))],
        out_specs=pl.BlockSpec((half, kc), lambda s: (0, 0)),
        out_shape=jax.ShapeDtypeStruct((half, kc), x.dtype),
        cost_estimate=cost(0, 4 * half * kc),
        compiler_params=pltpu.CompilerParams(vmem_limit_bytes=4 << 20),
    )(x)


def contract(pos, own, oth, blocks, half):
    rt, _, mi, kc = own.shape
    width = half * len(blocks)
    refs = [r for block in blocks for r in block]
    return pl.pallas_call(
        functools.partial(contract_kernel, half, tuple(len(block) for block in blocks)),
        in_specs=[SM] + [VM] * (2 + len(refs)),
        out_specs=VM,
        out_shape=jax.ShapeDtypeStruct((rt, 2, mi, width), BF),
        cost_estimate=cost(2 * 2 * rt * mi * 2 * kc * width, 2 * (4 * rt * mi * kc + width * 2 * kc + 2 * rt * mi * width)),
        compiler_params=pltpu.CompilerParams(vmem_limit_bytes=24 << 20),
    )(pos, own, oth, *refs)


def gather_sum_kernel(layout, half, z_ref, *refs):
    chunks, o_ref = refs[:-1], refs[-1]
    nz = o_ref.shape[0]
    for x_ref, offs in zip(chunks, layout):
        for core in range(x_ref.shape[1]):
            total = x_ref[0, core].astype(F32)
            for s in range(1, x_ref.shape[0]):
                total += x_ref[s, core].astype(F32)
            total = total.astype(BF)
            for b, off in enumerate(offs):
                at = lax.rem(z_ref[0] + off + nz, nz)
                o_ref[pl.ds(at, 1), core] = total[:, b * half : (b + 1) * half][None]


def antisym_kernel(pos_ref, occ_ref, slab_ref, s_ref, m_ref, o_ref):
    target = slab_ref[0] ^ slab_ref[1]
    n = s_ref.shape[2]
    side = 4
    r = lax.broadcasted_iota(jnp.int32, (n, 1), 0)
    ri = lax.broadcasted_iota(jnp.int32, (n, n), 0)
    ci = lax.broadcasted_iota(jnp.int32, (n, n), 1)
    swap = jnp.where((ri // side == ci % side) & (ri % side == ci // side), 1.0, 0.0).astype(BF)
    i_orb = pos_ref[0] * side + r // side
    j_orb = pos_ref[1] * side + r % side
    i_lab = jnp.zeros((n, 1), jnp.int32)
    j_lab = jnp.zeros((n, 1), jnp.int32)
    for k in range(1, 8):
        i_lab += (i_orb >= occ_ref[k]).astype(jnp.int32)
        j_lab += (j_orb >= occ_ref[k]).astype(jnp.int32)
    allowed = (i_lab ^ j_lab) == target
    for z in range(s_ref.shape[0]):
        for core in range(s_ref.shape[1]):
            flipped = jnp.dot(swap, m_ref[z, core], preferred_element_type=F32)
            mixed = s_ref[z, core].astype(F32) - flipped
            o_ref[z, core] = jnp.where(allowed, mixed, 0.0).astype(BF)


def assemble_kernel(p_ref, own_ref, oth_ref, o_ref):
    first = p_ref[0] == 0
    nj = o_ref.shape[1]

    def write(low_ref, high_ref):
        for i in range(o_ref.shape[0]):
            rows = slice(i * nj, (i + 1) * nj)
            parts = [
                ref[z, core, rows, :]
                for z in range(own_ref.shape[0])
                for core in range(own_ref.shape[1])
                for ref in (low_ref, high_ref)
            ]
            o_ref[i] = jnp.concatenate(parts, axis=1)

    @pl.when(first)
    def _():
        write(own_ref, oth_ref)

    @pl.when(jnp.logical_not(first))
    def _():
        write(oth_ref, own_ref)


def kernel_call(body, outs, in_specs, args, nbytes):
    many = isinstance(outs, (list, tuple))
    return pl.pallas_call(
        body,
        in_specs=in_specs,
        out_specs=[VM] * len(outs) if many else VM,
        out_shape=outs,
        cost_estimate=cost(nbytes, nbytes),
        compiler_params=pltpu.CompilerParams(vmem_limit_bytes=12 << 20),
    )(*args)


def residual_of(amplitudes, integrals, occ_offsets, slab):
    ni, nj, nk, nc = amplitudes.shape
    na, _, sub = integrals.shape
    rows = nc // sub
    half = na // 2
    kc = nk * sub

    def at(*axes):
        place = 0
        for axis in axes:
            place = place * lax.axis_size(axis) + lax.axis_index(axis)
        return place.astype(jnp.int32)

    def shift(x, axis, by):
        n = lax.axis_size(axis)
        return lax.ppermute(x, axis, [(d, (d + by) % n) for d in range(n)])

    mine = at("xl").reshape(1)
    padded = -(-half // 8) * 8
    keep, send = kernel_call(
        pack_b_kernel,
        [jax.ShapeDtypeStruct((padded, kc), BF)] * 2,
        [SM, VM],
        (mine, jnp.transpose(integrals, (1, 0, 2))),
        4 * na * kc,
    )
    packed_a = kernel_call(
        functools.partial(pack_a_kernel, rows, sub),
        jax.ShapeDtypeStruct((rows, 2, ni * nj, kc), BF),
        [VM],
        (jnp.transpose(amplitudes, (0, 2, 1, 3)),),
        6 * ni * nj * nk * nc,
    )
    recv = shift(send, "xl", 1)

    ring = {}
    for way, by in (("up", 1), ("down", -1)):
        first = shift(keep, "z", by)
        second = shift(recv, "z", by)
        ring[way, 1] = kernel_call(
            join_kernel,
            jax.ShapeDtypeStruct((2, padded, kc), BF),
            [VM, VM],
            (first, second),
            8 * padded * kc,
        )
        for t in (2, 3):
            ring[way, t] = shift(ring[way, t - 1], "z", by)
    far = []
    for p, (way, by) in enumerate((("up", 1), ("down", -1))):
        part = take_half(ring[way, 3], p)
        far.append(shift(part, "z", by))

    own = lax.all_to_all(
        packed_a.reshape(rows * 2, ni * nj, kc), PLANE, split_axis=0, concat_axis=0, tiled=True
    ).reshape(rows, 2, ni * nj, kc)
    oth = shift(own, "core", 1)

    plan = (
        ((0, -1, 1, -2, 2), [(keep, recv)] + [(ring[way, t],) for t in (1, 2) for way in ("up", "down")]),
        ((-3, 3, 4), [(ring["up", 3],), (ring["down", 3],), tuple(far)]),
    )
    layout = [offs for offs, _ in plan]
    pos = jnp.stack([at("core"), at("xl")])
    pieces = []
    for _, blocks in plan:
        part = contract(pos, own, oth, blocks, half)
        _, _, n, width = part.shape
        part = part.reshape(rows * 2, n, width)
        part = lax.all_to_all(part, TARGET, split_axis=0, concat_axis=0, tiled=True)
        pieces.append(part.reshape(rows, 2, n, width))

    n = ni * nj
    held = jax.ShapeDtypeStruct((lax.axis_size("z"), 2, n, half), BF)
    nbytes = 2 * lax.axis_size("z") * 2 * n * half
    total = kernel_call(
        functools.partial(gather_sum_kernel, layout, half),
        held,
        [SM] + [VM] * len(pieces),
        (at("z").reshape(1), *pieces),
        rows * nbytes,
    )

    shape = tuple(lax.axis_size(a) for a in AXES)
    pairs = []
    for at_y, at_xh, at_z, at_core, at_xl in np.ndindex(*shape):
        here, there = (at_y, at_xh, at_z, at_core, at_xl), (at_z, at_core, at_y, at_xh, at_xl)
        pairs.append((int(np.ravel_multi_index(here, shape)), int(np.ravel_multi_index(there, shape))))
    mirrored = lax.ppermute(total, AXES, pairs)
    mixed = kernel_call(
        antisym_kernel,
        held,
        [SM, SM, SM, VM, VM],
        (jnp.stack([at(*ROW), at("z", "core")]), occ_offsets, slab, total, mirrored),
        3 * nbytes,
    )
    other = shift(mixed, "xl", 1)
    return kernel_call(
        assemble_kernel,
        jax.ShapeDtypeStruct((ni, nj, lax.axis_size("z") * 4 * half), BF),
        [SM, VM, VM],
        (mine, mixed, other),
        4 * nbytes,
    )


def solution(mesh):
    fine = Mesh(mesh.devices.reshape(8, 2, 8, 2, 2), AXES)
    row, col = ROW, ("z", "core")
    placed = (P(row, col, "xl", None), P(col, "xl", row), P(), P())
    return jax.shard_map(
        residual_of, mesh=fine, in_specs=placed, out_specs=P(row, col, None), check_vma=False
    )
```

```python
import functools

import jax
import jax.numpy as jnp
import numpy as np
from jax import lax
from jax.experimental import pallas as pl
from jax.experimental.pallas import tpu as pltpu
from jax.sharding import Mesh, PartitionSpec as P

BF = jnp.bfloat16
F32 = jnp.float32
AXES = ("y", "xh", "z", "core", "xl")
ROW = ("xh", "y")
TARGET = ("xh", "y", "core")
VM = pl.BlockSpec(memory_space=pltpu.VMEM)
SM = pl.BlockSpec(memory_space=pltpu.SMEM)


def cost(flops, nbytes):
    return pl.CostEstimate(flops=flops, bytes_accessed=nbytes, transcendentals=0)


def pack_a_kernel(rows, sub, a_ref, o_ref):
    ni, nk, nj, _ = a_ref.shape
    for slot in range(rows):
        r = slot % (rows // 2) * 2 + slot // (rows // 2)
        for i in range(ni):
            piece = jnp.concatenate([a_ref[i, k, :, r * sub : (r + 1) * sub] for k in range(nk)], axis=1)
            o_ref[slot, i * nj : (i + 1) * nj, :] = piece


def pack_b_kernel(p_ref, b_ref, keep_ref, send_ref):
    full = jnp.concatenate([b_ref[k] for k in range(b_ref.shape[0])], axis=1)
    half = full.shape[0] // 2
    pad = jnp.zeros((keep_ref.shape[0] - half, full.shape[1]), full.dtype)
    low = jnp.concatenate([full[:half], pad], axis=0)
    high = jnp.concatenate([full[half:], pad], axis=0)
    first = p_ref[0] == 0

    @pl.when(first)
    def _():
        keep_ref[...] = low
        send_ref[...] = high

    @pl.when(jnp.logical_not(first))
    def _():
        keep_ref[...] = high
        send_ref[...] = low


def join_kernel(x_ref, y_ref, o_ref):
    o_ref[0] = x_ref[...]
    o_ref[1] = y_ref[...]


def contract_kernel(half, count, core_ref, own0, own1, oth0, oth1, *refs):
    blocks, earlier, o_ref = refs[:count], refs[count:-1], refs[-1]
    core = core_ref[0]
    dims = (((1,), (1,)), ((), ()))
    rt, mi, kc = own0.shape
    for slot, pair in ((core, (own0, own1)), (1 - core, (oth0, oth1))):
        lhs = [ref[...].reshape(rt * mi, kc) for ref in pair]
        parts = [r[:, pl.ds(slot, 1)].reshape(rt * mi, r.shape[-1]) for r in earlier]
        for block in blocks:
            acc = lax.dot_general(lhs[0], block[0], dims, preferred_element_type=F32)
            acc += lax.dot_general(lhs[1], block[1], dims, preferred_element_type=F32)
            parts.append(acc[:, :half].astype(BF))
        full = parts[0] if len(parts) == 1 else jnp.concatenate(parts, axis=1)
        o_ref[:, pl.ds(slot, 1), :, :] = full.reshape(rt, 1, mi, full.shape[1])


def contract(core, amps, blocks, half, earlier=()):
    rt, mi, kc = amps[0].shape
    fresh = half * len(blocks)
    width = fresh + sum(e.shape[-1] for e in earlier)
    return pl.pallas_call(
        functools.partial(contract_kernel, half, len(blocks)),
        in_specs=[SM] + [VM] * (4 + len(blocks) + len(earlier)),
        out_specs=VM,
        out_shape=jax.ShapeDtypeStruct((rt, 2, mi, width), BF),
        cost_estimate=cost(2 * 2 * rt * mi * 2 * kc * fresh, 2 * (4 * rt * mi * kc + fresh * 2 * kc + 2 * rt * mi * width)),
        compiler_params=pltpu.CompilerParams(vmem_limit_bytes=24 << 20),
    )(core, *amps, *blocks, *earlier)


def total_kernel(half, x_ref, o_ref):
    sums = []
    for core in range(x_ref.shape[1]):
        acc = x_ref[0, core].astype(F32)
        for s in range(1, x_ref.shape[0]):
            acc += x_ref[s, core].astype(F32)
        sums.append(acc.astype(BF))
    for b in range(o_ref.shape[0]):
        o_ref[b] = jnp.concatenate([v[:, b * half : (b + 1) * half] for v in sums], axis=1)


def mask_kernel(y_ref, xh_ref, z_ref, core_ref, occ_ref, slab_ref, o_ref):
    target = slab_ref[0] ^ slab_ref[1]
    side = 4
    r = lax.broadcasted_iota(jnp.int32, o_ref.shape, 0)
    i_orb = (2 * y_ref[0] + xh_ref[0]) * side + r // side
    j_orb = (2 * z_ref[0] + core_ref[0]) * side + r % side
    i_lab = jnp.zeros(o_ref.shape, jnp.int32)
    j_lab = jnp.zeros(o_ref.shape, jnp.int32)
    for k in range(1, 8):
        i_lab += (i_orb >= occ_ref[k]).astype(jnp.int32)
        j_lab += (j_orb >= occ_ref[k]).astype(jnp.int32)
    o_ref[...] = ((i_lab ^ j_lab) == target).astype(jnp.int32)


def split_total_kernel(half, core_ref, x_ref, keep_ref, send_ref):
    for slot, o_ref in ((core_ref[0], keep_ref), (1 - core_ref[0], send_ref)):
        acc = x_ref[0, pl.ds(slot, 1)].astype(F32)
        for s in range(1, x_ref.shape[0]):
            acc += x_ref[s, pl.ds(slot, 1)].astype(F32)
        acc = acc[0].astype(BF)
        for b in range(o_ref.shape[0]):
            o_ref[b] = acc[:, b * half : (b + 1) * half]


def pair_kernel(core_ref, own_ref, oth_ref, o_ref):
    first = core_ref[0] == 0

    @pl.when(first)
    def _():
        o_ref[...] = jnp.concatenate([own_ref[...], oth_ref[...]], axis=2)

    @pl.when(jnp.logical_not(first))
    def _():
        o_ref[...] = jnp.concatenate([oth_ref[...], own_ref[...]], axis=2)


def antisym_kernel(layout, y_ref, z_ref, mask_ref, *refs):
    chunks = len(layout)
    s_refs, m_refs = refs[:chunks], refs[chunks : 2 * chunks]
    o_ref, s_all, m_all = refs[2 * chunks :]
    nz, n, _ = o_ref.shape
    for all_ref, parts, origin in ((s_all, s_refs, z_ref[0]), (m_all, m_refs, y_ref[0])):
        for offs, ref in zip(layout, parts):
            for b, off in enumerate(offs):
                all_ref[pl.ds(lax.rem(origin + off + nz, nz), 1)] = ref[b][None]
    side = 4
    ri = lax.broadcasted_iota(jnp.int32, (n, n), 0)
    ci = lax.broadcasted_iota(jnp.int32, (n, n), 1)
    swap = jnp.where((ri // side == ci % side) & (ri % side == ci // side), 1.0, 0.0).astype(BF)
    allowed = mask_ref[:, :1] > 0
    for z in range(nz):
        flipped = jnp.dot(swap, m_all[z], preferred_element_type=F32)
        mixed = s_all[z].astype(F32) - flipped
        o_ref[z] = jnp.where(allowed, mixed, 0.0).astype(BF)


def assemble_kernel(half, p_ref, own_ref, oth_ref, o_ref):
    first = p_ref[0] == 0
    nj = o_ref.shape[1]

    def write(low_ref, high_ref):
        for i in range(o_ref.shape[0]):
            rows = slice(i * nj, (i + 1) * nj)
            parts = [
                ref[z, rows, core * half : (core + 1) * half]
                for z in range(own_ref.shape[0])
                for core in range(2)
                for ref in (low_ref, high_ref)
            ]
            o_ref[i] = jnp.concatenate(parts, axis=1)

    @pl.when(first)
    def _():
        write(own_ref, oth_ref)

    @pl.when(jnp.logical_not(first))
    def _():
        write(oth_ref, own_ref)


def kernel_call(body, outs, in_specs, args, nbytes, scratch=()):
    many = isinstance(outs, (list, tuple))
    return pl.pallas_call(
        body,
        in_specs=in_specs,
        out_specs=[VM] * len(outs) if many else VM,
        out_shape=outs,
        scratch_shapes=scratch,
        cost_estimate=cost(nbytes, nbytes),
        compiler_params=pltpu.CompilerParams(vmem_limit_bytes=12 << 20),
    )(*args)


def residual_of(amplitudes, integrals, occ_offsets, slab):
    ni, nj, nk, nc = amplitudes.shape
    na, _, sub = integrals.shape
    rows = nc // sub
    half = na // 2
    kc = nk * sub

    def at(axis):
        return lax.axis_index(axis).astype(jnp.int32).reshape(1)

    def shift(x, axis, by):
        n = lax.axis_size(axis)
        return lax.ppermute(x, axis, [(d, (d + by) % n) for d in range(n)])

    padded = -(-half // 8) * 8
    keep, send = kernel_call(
        pack_b_kernel,
        [jax.ShapeDtypeStruct((padded, kc), BF)] * 2,
        [SM, VM],
        (at("xl"), jnp.transpose(integrals, (1, 0, 2))),
        4 * na * kc,
    )
    packed_a = kernel_call(
        functools.partial(pack_a_kernel, rows, sub),
        jax.ShapeDtypeStruct((rows, ni * nj, kc), BF),
        [VM],
        (jnp.transpose(amplitudes, (0, 2, 1, 3)),),
        4 * ni * nj * nk * nc,
    )
    recv = shift(send, "xl", 1)

    block = kernel_call(
        join_kernel,
        jax.ShapeDtypeStruct((2, padded, kc), BF),
        [VM, VM],
        (keep, recv),
        8 * padded * kc,
    )

    up, down = [block], [block]
    for t in range(1, 5):
        up.append(shift(up[-1], "z", 1))
        if t < 4:
            down.append(shift(down[-1], "z", -1))

    own0 = lax.all_to_all(packed_a, ROW, split_axis=0, concat_axis=0, tiled=True)
    own1 = shift(own0, "xl", 1)
    oth0 = shift(own0, "core", 1)
    oth1 = shift(own1, "core", 1)

    layout = ((0, -1, 1, -2, 2), (-3, 4, 3))
    where, amps = at("core"), (own0, own1, oth0, oth1)
    near = contract(where, amps, (block, up[1], down[1]), half)
    part_0 = contract(where, amps, (up[2], down[2]), half, (near,))
    early = contract(where, amps, (up[3], up[4]), half)
    part_1 = contract(where, amps, (down[3],), half, (early,))

    n = ni * nj
    shape = tuple(lax.axis_size(a) for a in AXES)
    pairs = []
    for at_y, at_xh, at_z, at_core, at_xl in np.ndindex(*shape):
        here, there = (at_y, at_xh, at_z, at_core, at_xl), (at_z, at_core, at_y, at_xh, at_xl)
        pairs.append((int(np.ravel_multi_index(here, shape)), int(np.ravel_multi_index(there, shape))))
    sums, mirrored = [], []
    blocks, width = len(layout[0]), part_0.shape[-1]
    part_0 = lax.all_to_all(part_0, ROW, split_axis=0, concat_axis=0, tiled=True)
    mine, theirs = kernel_call(
        functools.partial(split_total_kernel, half),
        [jax.ShapeDtypeStruct((blocks, n, half), BF)] * 2,
        [SM, VM],
        (where, part_0),
        4 * rows * n * width,
    )
    given = shift(theirs, "core", 1)
    sums.append(
        kernel_call(
            pair_kernel,
            jax.ShapeDtypeStruct((blocks, n, 2 * half), BF),
            [SM, VM, VM],
            (where, mine, given),
            8 * blocks * n * half,
        )
    )
    blocks, width = len(layout[1]), part_1.shape[-1]
    part_1 = part_1.reshape(rows * 2, n, width)
    part_1 = lax.all_to_all(part_1, TARGET, split_axis=0, concat_axis=0, tiled=True)
    part_1 = part_1.reshape(rows, 2, n, width)
    sums.append(
        kernel_call(
            functools.partial(total_kernel, half),
            jax.ShapeDtypeStruct((blocks, n, 2 * half), BF),
            [VM],
            (part_1,),
            4 * rows * n * width,
        )
    )
    for c in range(2):
        mirrored.append(lax.ppermute(sums[c], AXES, pairs))

    held = (lax.axis_size("z"), n, 2 * half)
    allowed = kernel_call(
        mask_kernel,
        jax.ShapeDtypeStruct((n, 128), jnp.int32),
        [SM] * 6,
        (at("y"), at("xh"), at("z"), at("core"), occ_offsets, slab),
        4 * n * 128,
    )
    mixed = kernel_call(
        functools.partial(antisym_kernel, layout),
        jax.ShapeDtypeStruct(held, BF),
        [SM] * 2 + [VM] * 5,
        (at("y"), at("z"), allowed, *sums, *mirrored),
        6 * int(np.prod(held)),
        [pltpu.VMEM(held, BF)] * 2,
    )
    other = shift(mixed, "xl", 1)
    return kernel_call(
        functools.partial(assemble_kernel, half),
        jax.ShapeDtypeStruct((ni, nj, held[0] * 4 * half), BF),
        [SM, VM, VM],
        (at("xl"), mixed, other),
        8 * int(np.prod(held)),
    )


def solution(mesh):
    fine = Mesh(mesh.devices.reshape(8, 2, 8, 2, 2), AXES)
    row, col = ("y", "xh"), ("z", "core")
    placed = (P(row, col, "xl", None), P(col, "xl", row), P(), P())
    return jax.shard_map(
        residual_of, mesh=fine, in_specs=placed, out_specs=P(row, col, None), check_vma=False
    )
```

```python
import functools

import jax
import jax.numpy as jnp
import numpy as np
from jax import lax
from jax.experimental import pallas as pl
from jax.experimental.pallas import tpu as pltpu
from jax.sharding import Mesh, PartitionSpec as P

BF = jnp.bfloat16
F32 = jnp.float32
AXES = ("y", "xh", "z", "core", "xl")
ROW = ("xh", "y")
TARGET = ("xh", "y", "core")
VM = pl.BlockSpec(memory_space=pltpu.VMEM)
SM = pl.BlockSpec(memory_space=pltpu.SMEM)


def cost(flops, nbytes):
    return pl.CostEstimate(flops=flops, bytes_accessed=nbytes, transcendentals=0)


def pack_a_kernel(rows, sub, a_ref, o_ref):
    ni, nk, nj, _ = a_ref.shape
    for slot in range(rows):
        r = slot % (rows // 2) * 2 + slot // (rows // 2)
        for i in range(ni):
            piece = jnp.concatenate([a_ref[i, k, :, r * sub : (r + 1) * sub] for k in range(nk)], axis=1)
            o_ref[slot, i * nj : (i + 1) * nj, :] = piece


def pack_b_kernel(p_ref, b_ref, keep_ref, send_ref):
    full = jnp.concatenate([b_ref[k] for k in range(b_ref.shape[0])], axis=1)
    half = full.shape[0] // 2
    pad = jnp.zeros((keep_ref.shape[0] - half, full.shape[1]), full.dtype)
    low = jnp.concatenate([full[:half], pad], axis=0)
    high = jnp.concatenate([full[half:], pad], axis=0)
    first = p_ref[0] == 0

    @pl.when(first)
    def _():
        keep_ref[...] = low
        send_ref[...] = high

    @pl.when(jnp.logical_not(first))
    def _():
        keep_ref[...] = high
        send_ref[...] = low


def block_plan(half, kc):
    whole = kc // 128 * 128
    second = 128 - kc % 128
    left = kc - whole - second
    top = half // 8 * 8
    spare = top + 8 - half
    return whole, second, left, top, spare


def spread(half, kc, first_axis):
    _, _, left, _, spare = block_plan(half, kc)
    slots = -(-left // spare) * 8
    shape = (left, slots) if first_axis else (slots, left)
    source = lax.broadcasted_iota(jnp.int32, shape, 0 if first_axis else 1)
    slot = lax.broadcasted_iota(jnp.int32, shape, 1 if first_axis else 0)
    hit = slot == source // spare * 8 + (8 - spare) + source % spare
    return jnp.where(hit, 1.0, 0.0).astype(BF)


def join_kernel(half, x_ref, y_ref, o_ref):
    rows, kc = x_ref.shape
    whole, second, _, top, _ = block_plan(half, kc)
    wide = whole + second
    x, y = x_ref[...], y_ref[...]
    main = jnp.concatenate([x, y[:, whole:wide], y[:, :whole]], axis=1)
    o_ref[:top] = main[:top]
    dims = (((1,), (1,)), ((), ()))
    turned = lax.dot_general(spread(half, kc, False), y[:, wide:], dims, preferred_element_type=F32)
    bottom = main[top:].astype(F32)
    gap = jnp.zeros((8, -rows % 128), F32)
    parts = []
    for g in range(turned.shape[0] // 8):
        parts += [turned[g * 8 : (g + 1) * 8], gap]
    parts.append(jnp.zeros((8, main.shape[1] - sum(v.shape[1] for v in parts)), F32))
    o_ref[top:] = (bottom + jnp.concatenate(parts, axis=1)).astype(BF)


def contract_kernel(half, count, core_ref, own0, own1, oth0, oth1, *refs):
    blocks, earlier, o_ref = refs[:count], refs[count:-1], refs[-1]
    core = core_ref[0]
    dims = (((1,), (1,)), ((), ()))
    rt, mi, kc = own0.shape
    whole, second, left, top, spare = block_plan(half, kc)
    wide = whole + second
    rows = top + 8
    step = rows + -rows % 128
    groups = -(-left // spare)
    for slot, pair in ((core, (own0, own1)), (1 - core, (oth0, oth1))):
        lhs0, lhs1 = [ref[...].reshape(rt * mi, kc) for ref in pair]
        front = jnp.concatenate([lhs0, lhs1[:, whole:wide]], axis=1)
        back = lhs1[:, :whole]
        last = jnp.dot(lhs1[:, wide:], spread(half, kc, True), preferred_element_type=F32).astype(BF)
        parts = [r[:, pl.ds(slot, 1)].reshape(rt * mi, r.shape[-1]) for r in earlier]
        for block in blocks:
            turned = [block[top:, g * step : g * step + rows].astype(F32) for g in range(groups)]
            turned = jnp.concatenate(turned, axis=0).astype(BF)
            acc = lax.dot_general(front, block[:, : whole + 128], dims, preferred_element_type=F32)
            acc += lax.dot_general(back, block[:, whole + 128 :], dims, preferred_element_type=F32)
            acc += jnp.dot(last, turned, preferred_element_type=F32)
            parts.append(acc[:, :half].astype(BF))
        full = parts[0] if len(parts) == 1 else jnp.concatenate(parts, axis=1)
        o_ref[:, pl.ds(slot, 1), :, :] = full.reshape(rt, 1, mi, full.shape[1])


def contract(core, amps, blocks, half, earlier=()):
    rt, mi, kc = amps[0].shape
    fresh = half * len(blocks)
    width = fresh + sum(e.shape[-1] for e in earlier)
    return pl.pallas_call(
        functools.partial(contract_kernel, half, len(blocks)),
        in_specs=[SM] + [VM] * (4 + len(blocks) + len(earlier)),
        out_specs=VM,
        out_shape=jax.ShapeDtypeStruct((rt, 2, mi, width), BF),
        cost_estimate=cost(2 * 2 * rt * mi * 2 * kc * fresh, 2 * (4 * rt * mi * kc + fresh * 2 * kc + 2 * rt * mi * width)),
        compiler_params=pltpu.CompilerParams(vmem_limit_bytes=24 << 20),
    )(core, *amps, *blocks, *earlier)


def total_kernel(half, x_ref, o_ref):
    sums = []
    for core in range(x_ref.shape[1]):
        acc = x_ref[0, core].astype(F32)
        for s in range(1, x_ref.shape[0]):
            acc += x_ref[s, core].astype(F32)
        sums.append(acc.astype(BF))
    for b in range(o_ref.shape[0]):
        o_ref[b] = jnp.concatenate([v[:, b * half : (b + 1) * half] for v in sums], axis=1)


def mask_kernel(y_ref, xh_ref, z_ref, core_ref, occ_ref, slab_ref, o_ref):
    target = slab_ref[0] ^ slab_ref[1]
    side = 4
    r = lax.broadcasted_iota(jnp.int32, o_ref.shape, 0)
    i_orb = (2 * y_ref[0] + xh_ref[0]) * side + r // side
    j_orb = (2 * z_ref[0] + core_ref[0]) * side + r % side
    i_lab = jnp.zeros(o_ref.shape, jnp.int32)
    j_lab = jnp.zeros(o_ref.shape, jnp.int32)
    for k in range(1, 8):
        i_lab += (i_orb >= occ_ref[k]).astype(jnp.int32)
        j_lab += (j_orb >= occ_ref[k]).astype(jnp.int32)
    o_ref[...] = ((i_lab ^ j_lab) == target).astype(jnp.int32)


def split_total_kernel(half, core_ref, x_ref, keep_ref, send_ref):
    for slot, o_ref in ((core_ref[0], keep_ref), (1 - core_ref[0], send_ref)):
        acc = x_ref[0, pl.ds(slot, 1)].astype(F32)
        for s in range(1, x_ref.shape[0]):
            acc += x_ref[s, pl.ds(slot, 1)].astype(F32)
        acc = acc[0].astype(BF)
        for b in range(o_ref.shape[0]):
            o_ref[b] = acc[:, b * half : (b + 1) * half]


def pair_kernel(core_ref, own_ref, oth_ref, o_ref):
    first = core_ref[0] == 0

    @pl.when(first)
    def _():
        o_ref[...] = jnp.concatenate([own_ref[...], oth_ref[...]], axis=2)

    @pl.when(jnp.logical_not(first))
    def _():
        o_ref[...] = jnp.concatenate([oth_ref[...], own_ref[...]], axis=2)


def antisym_kernel(layout, y_ref, z_ref, mask_ref, *refs):
    chunks = len(layout)
    s_refs, m_refs = refs[:chunks], refs[chunks : 2 * chunks]
    o_ref, s_all, m_all = refs[2 * chunks :]
    nz, n, _ = o_ref.shape
    for all_ref, parts, origin in ((s_all, s_refs, z_ref[0]), (m_all, m_refs, y_ref[0])):
        for offs, ref in zip(layout, parts):
            for b, off in enumerate(offs):
                all_ref[pl.ds(lax.rem(origin + off + nz, nz), 1)] = ref[b][None]
    side = 4
    ri = lax.broadcasted_iota(jnp.int32, (n, n), 0)
    ci = lax.broadcasted_iota(jnp.int32, (n, n), 1)
    swap = jnp.where((ri // side == ci % side) & (ri % side == ci // side), 1.0, 0.0).astype(BF)
    allowed = mask_ref[:, :1] > 0
    for z in range(nz):
        flipped = jnp.dot(swap, m_all[z], preferred_element_type=F32)
        mixed = s_all[z].astype(F32) - flipped
        o_ref[z] = jnp.where(allowed, mixed, 0.0).astype(BF)


def assemble_kernel(half, p_ref, own_ref, oth_ref, o_ref):
    first = p_ref[0] == 0
    nj = o_ref.shape[1]

    def write(low_ref, high_ref):
        for i in range(o_ref.shape[0]):
            rows = slice(i * nj, (i + 1) * nj)
            parts = [
                ref[z, rows, core * half : (core + 1) * half]
                for z in range(own_ref.shape[0])
                for core in range(2)
                for ref in (low_ref, high_ref)
            ]
            o_ref[i] = jnp.concatenate(parts, axis=1)

    @pl.when(first)
    def _():
        write(own_ref, oth_ref)

    @pl.when(jnp.logical_not(first))
    def _():
        write(oth_ref, own_ref)


def kernel_call(body, outs, in_specs, args, nbytes, scratch=()):
    many = isinstance(outs, (list, tuple))
    return pl.pallas_call(
        body,
        in_specs=in_specs,
        out_specs=[VM] * len(outs) if many else VM,
        out_shape=outs,
        scratch_shapes=scratch,
        cost_estimate=cost(nbytes, nbytes),
        compiler_params=pltpu.CompilerParams(vmem_limit_bytes=12 << 20),
    )(*args)


def residual_of(amplitudes, integrals, occ_offsets, slab):
    ni, nj, nk, nc = amplitudes.shape
    na, _, sub = integrals.shape
    rows = nc // sub
    half = na // 2
    kc = nk * sub

    def at(axis):
        return lax.axis_index(axis).astype(jnp.int32).reshape(1)

    def shift(x, axis, by):
        n = lax.axis_size(axis)
        return lax.ppermute(x, axis, [(d, (d + by) % n) for d in range(n)])

    padded = -(-half // 8) * 8
    keep, send = kernel_call(
        pack_b_kernel,
        [jax.ShapeDtypeStruct((padded, kc), BF)] * 2,
        [SM, VM],
        (at("xl"), jnp.transpose(integrals, (1, 0, 2))),
        4 * na * kc,
    )
    packed_a = kernel_call(
        functools.partial(pack_a_kernel, rows, sub),
        jax.ShapeDtypeStruct((rows, ni * nj, kc), BF),
        [VM],
        (jnp.transpose(amplitudes, (0, 2, 1, 3)),),
        4 * ni * nj * nk * nc,
    )
    recv = shift(send, "xl", 1)

    block = kernel_call(
        functools.partial(join_kernel, half),
        jax.ShapeDtypeStruct((padded, 2 * (kc // 128 * 128) + 128), BF),
        [VM, VM],
        (keep, recv),
        8 * padded * kc,
    )

    up, down = [block], [block]
    for t in range(1, 5):
        up.append(shift(up[-1], "z", 1))
        if t < 4:
            down.append(shift(down[-1], "z", -1))

    own0 = lax.all_to_all(packed_a, ROW, split_axis=0, concat_axis=0, tiled=True)
    own1 = shift(own0, "xl", 1)
    oth0 = shift(own0, "core", 1)
    oth1 = shift(own1, "core", 1)

    layout = ((0, -1, 1, -2, 2), (-3, 3, 4))
    where, amps = at("core"), (own0, own1, oth0, oth1)
    near = contract(where, amps, (block, up[1], down[1]), half)
    part_0 = contract(where, amps, (up[2], down[2]), half, (near,))
    early = contract(where, amps, (up[3], down[3]), half)
    part_1 = contract(where, amps, (up[4],), half, (early,))

    n = ni * nj
    shape = tuple(lax.axis_size(a) for a in AXES)
    pairs = []
    for at_y, at_xh, at_z, at_core, at_xl in np.ndindex(*shape):
        here, there = (at_y, at_xh, at_z, at_core, at_xl), (at_z, at_core, at_y, at_xh, at_xl)
        pairs.append((int(np.ravel_multi_index(here, shape)), int(np.ravel_multi_index(there, shape))))
    sums, mirrored = [], []
    blocks, width = len(layout[0]), part_0.shape[-1]
    part_0 = lax.all_to_all(part_0, ROW, split_axis=0, concat_axis=0, tiled=True)
    mine, theirs = kernel_call(
        functools.partial(split_total_kernel, half),
        [jax.ShapeDtypeStruct((blocks, n, half), BF)] * 2,
        [SM, VM],
        (where, part_0),
        4 * rows * n * width,
    )
    given = shift(theirs, "core", 1)
    sums.append(
        kernel_call(
            pair_kernel,
            jax.ShapeDtypeStruct((blocks, n, 2 * half), BF),
            [SM, VM, VM],
            (where, mine, given),
            8 * blocks * n * half,
        )
    )
    blocks, width = len(layout[1]), part_1.shape[-1]
    part_1 = part_1.reshape(rows * 2, n, width)
    part_1 = lax.all_to_all(part_1, TARGET, split_axis=0, concat_axis=0, tiled=True)
    part_1 = part_1.reshape(rows, 2, n, width)
    sums.append(
        kernel_call(
            functools.partial(total_kernel, half),
            jax.ShapeDtypeStruct((blocks, n, 2 * half), BF),
            [VM],
            (part_1,),
            4 * rows * n * width,
        )
    )
    for c in range(2):
        mirrored.append(lax.ppermute(sums[c], AXES, pairs))

    held = (lax.axis_size("z"), n, 2 * half)
    allowed = kernel_call(
        mask_kernel,
        jax.ShapeDtypeStruct((n, 128), jnp.int32),
        [SM] * 6,
        (at("y"), at("xh"), at("z"), at("core"), occ_offsets, slab),
        4 * n * 128,
    )
    mixed = kernel_call(
        functools.partial(antisym_kernel, layout),
        jax.ShapeDtypeStruct(held, BF),
        [SM] * 2 + [VM] * 5,
        (at("y"), at("z"), allowed, *sums, *mirrored),
        6 * int(np.prod(held)),
        [pltpu.VMEM(held, BF)] * 2,
    )
    other = shift(mixed, "xl", 1)
    return kernel_call(
        functools.partial(assemble_kernel, half),
        jax.ShapeDtypeStruct((ni, nj, held[0] * 4 * half), BF),
        [SM, VM, VM],
        (at("xl"), mixed, other),
        8 * int(np.prod(held)),
    )


def solution(mesh):
    fine = Mesh(mesh.devices.reshape(8, 2, 8, 2, 2), AXES)
    row, col = ("y", "xh"), ("z", "core")
    placed = (P(row, col, "xl", None), P(col, "xl", row), P(), P())
    return jax.shard_map(
        residual_of, mesh=fine, in_specs=placed, out_specs=P(row, col, None), check_vma=False
    )
```
